128 devices in a mesh: expert: 4 (over y), seq: 32 (over z, x, core).
Axes of the slice: x: 4, y: 4, z: 4, core: 2. Of those that a mesh axis runs over, the one named last changes fastest.
Arguments:
- moe_input: bfloat16 [32, 256, 2048], P('seq', 'expert'), may hold values from -6 to 6
- out_grad: bfloat16 [32, 256, 2048], P('seq', 'expert'), may hold values from -6 to 6
- expert_id: int32 [32, 256, 1], P('seq', 'expert'), may hold values from 0 to 7; in each aligned block of 64 rows (0 to 63, 64 to 127, ..., all dimensions but the last counted through in order) at most 10 rows name the same one
- w_gate: bfloat16 [8, 2048, 8192], P('expert', None, 'seq'), may hold values from -0.125 to 0.125
- w_up: bfloat16 [8, 2048, 8192], P('expert', None, 'seq'), may hold values from -0.125 to 0.125
- w_down: bfloat16 [8, 8192, 2048], P('expert', 'seq'), may hold values from -0.0625 to 0.0625
- w_out: bfloat16 [4096, 2048], P('expert'), may hold values from -0.09375 to 0.09375
- b_proj: bfloat16 [32, 256, 128], P('seq'), may hold values from -6 to 6
- c_proj: bfloat16 [32, 256, 128], P('seq'), may hold values from -0.046875 to 0.046875
- log_decay: float32 [32, 64, 256], P('seq', 'expert'), may hold values from -0.7 to 0, as said below
Outputs:
- head_grad: bfloat16 [32, 256, 4096], P('seq', None, 'expert')
- input_grad: bfloat16 [32, 256, 2048], P('seq', 'expert')
- gate_grad: float32 [8, 2048, 8192], P('expert', None, 'seq')
- up_grad: float32 [8, 2048, 8192], P('expert', None, 'seq')
- down_grad: float32 [8, 8192, 2048], P('expert', 'seq')
The draws below stay inside these ranges and needn't reach their ends.
Inputs may be any that keep to these rules, and one draw needn't show every extreme that they name: `expert_id`: at most 10 tokens of one aligned block of 64 tokens (one device's tokens) name the same expert, and some block reaches 10. `log_decay`: Negative.
All inputs are finite; a program needn't handle non-finite values.
Results may differ from the reference program's by a relative error of at most 0.019.
Values may be sent and summed in bfloat16 or wider, within the bound.
No kernel may reach another device: no remote copies, remote signals or barrier semaphores. Data moves between devices by JAX's collectives and lax.ppermute only.
A program may use at most 192 MiB of HBM per device.

```python
import math
import jax
import jax.numpy as jnp
import numpy as np
from jax import lax

D = 2048
FF = 8192
RECURRENT_LANES = 64
P_SIZE = 64
N = 128
TOK_DEV = 64
CAP = 10
PIECE_LENGTH = 256
SPAN_PARTITIONS = 32
EXPERTS = 8
TOKENS = 8192
N_EXPERT = 4
N_SEQ = 32


def draw_log_decay(key, part):
    streams = jax.random.split(key, 7)
    total = SPAN_PARTITIONS * PIECE_LENGTH
    fast_share = 0.5
    fast = jax.random.uniform(streams[0], (1, RECURRENT_LANES, 1)) < fast_share
    fast_rate = jax.random.uniform(streams[1], (1, RECURRENT_LANES, 1), minval=1.0 / 50.0, maxval=1.0 / 30.0)
    slow_rate = jax.random.uniform(streams[2], (1, RECURRENT_LANES, 1), minval=0.15, maxval=0.6) / total
    device_factor = jnp.exp(jax.random.uniform(streams[3], (SPAN_PARTITIONS, RECURRENT_LANES, 1), minval=-0.35, maxval=0.35))
    token_factor = jax.random.uniform(streams[4], (SPAN_PARTITIONS, RECURRENT_LANES, PIECE_LENGTH), minval=0.5, maxval=1.5)
    fading_speeds = jnp.where(fast, fast_rate, slow_rate) * device_factor * token_factor
    expert_locations = jax.random.randint(streams[5], (2,), 0, total)
    surviving_entries = jax.random.uniform(streams[6], (2, RECURRENT_LANES), minval=0.55, maxval=0.8)
    element_offset = (jnp.arange(SPAN_PARTITIONS)[:, None] * PIECE_LENGTH + jnp.arange(PIECE_LENGTH)[None, :])[:, None, :]
    spike_occurrences = jnp.zeros((SPAN_PARTITIONS, RECURRENT_LANES, PIECE_LENGTH), jnp.float32)
    for chosen_expert_number in range(2):
        spike_occurrences = spike_occurrences + jnp.where(element_offset == expert_locations[chosen_expert_number], jnp.log(surviving_entries[chosen_expert_number])[None, :, None], 0.0)
    return (spike_occurrences - fading_speeds).astype(jnp.float32)


def block_levels(key, extent, cuts, smallest, top_value):
    loudness, own = 1.0, jax.random.fold_in(key, 6)
    for axis_at, blocks in cuts:
        steps = jnp.exp(jax.random.uniform(jax.random.fold_in(own, axis_at), (blocks,), jnp.float32, smallest / len(cuts), top_value / len(cuts)))
        loudness = loudness * jnp.repeat(steps, extent[axis_at] // blocks).reshape([-1 if axis == axis_at else 1 for axis in range(len(extent))])
    return loudness


def deal_out(rng, own, number, rows, number_of, top, bound, lean):
    sequence = jax.random.permutation(rng, number_of)
    heavy_load, ordinary = shares(number_of, rows * top, bound, lean, True), shares(number_of, rows * top, bound, lean, False)
    places = jnp.arange(number_of)

    def named(lengths, turn):
        used = int((lengths > 0).sum())
        fixed = max(1, used // 4)
        passed = fixed + (places - fixed + turn * (used - fixed)) % max(1, number_of - fixed)
        return jnp.zeros((number_of,), jnp.int32).at[sequence[jnp.where(places < fixed, places, passed)]].set(jnp.asarray(lengths, jnp.int32))

    lengths = jnp.where(number % 4 == 0, named(heavy_load, number // 4), named(ordinary, number - number // 4 - 1))
    mixed = jax.random.permutation(jax.random.fold_in(own, 3), number_of)
    donor, taker = mixed[0:number_of // 2 * 2:2], mixed[1:number_of // 2 * 2:2]
    margin = jnp.minimum(lengths[donor] - 1, bound - lengths[taker]) // 2
    margin = jnp.where((donor == sequence[0]) | (taker == sequence[0]) | (lengths[taker] == 0), 0, jnp.maximum(margin, 0))
    passed = jax.random.randint(jax.random.fold_in(own, 4), (number_of // 2,), 0, 1 << 20) % (margin + 1)
    lengths = lengths.at[donor].add(-passed).at[taker].add(passed)
    items = jnp.searchsorted(jnp.cumsum(lengths), jnp.arange(rows * top), side="right").astype(jnp.int32)
    listing = items.reshape(top, rows).T
    listing = listing[jax.random.permutation(jax.random.fold_in(own, 1), rows)]
    turn = jax.random.randint(jax.random.fold_in(own, 2), (rows, 1), 0, top)
    return jnp.take_along_axis(listing, (jnp.arange(top)[None, :] + turn) % top, axis=1)


def shares(number_of, total, limit, lean, full):
    loads = [(1 << 20) // math.isqrt(rank ** lean) + 1 for rank in range(1, number_of + 1)]
    largest = limit if full else min(limit, max(-(-total // number_of), total * loads[0] // sum(loads)))
    least = 1 if total - largest >= number_of - 1 else 0
    given, rest = [largest] + [least] * (number_of - 1), total - largest - least * (number_of - 1)
    while rest > 0:
        movable = [i for i in range(1, number_of) if given[i] < largest] or [i for i in range(1, number_of) if given[i] < limit]
        whole, remaining = sum([loads[i] for i in movable]), rest
        for i in movable:
            more = min(limit - given[i], max(1, remaining * loads[i] // whole), rest)
            given[i] = given[i] + more
            rest = rest - more
    return np.array(given)


def centred(own_key, shape, scale, limit, cuts=(), kind=jnp.bfloat16):
    array = scale * jax.random.normal(own_key, shape, jnp.float32)
    if cuts:
        array = array * block_levels(own_key, shape, cuts, -0.22, 0.18)
    return jnp.clip(array, -limit, limit).astype(kind)


def setup_inputs(seed: int = 0) -> dict:
    key_of = jax.random.split(jax.random.key(seed), 11)
    moe_input = centred(key_of[0], (SPAN_PARTITIONS, PIECE_LENGTH, D), 1.0, 6.0, ((0, 32), (1, 4)))
    out_grad = centred(key_of[1], (SPAN_PARTITIONS, PIECE_LENGTH, D), 1.0, 6.0, ((0, 32), (1, 4)))
    expert_id_keys = jax.random.split(jax.random.fold_in(key_of[2], 1), SPAN_PARTITIONS * PIECE_LENGTH // TOK_DEV)
    expert_id_turns = jax.random.permutation(jax.random.fold_in(key_of[2], 3), SPAN_PARTITIONS * PIECE_LENGTH // TOK_DEV)
    expert_id = jax.vmap(lambda own, number: deal_out(jax.random.fold_in(key_of[2], 2), own, number, TOK_DEV, EXPERTS, 1, CAP, 1))(expert_id_keys, expert_id_turns).reshape((SPAN_PARTITIONS, PIECE_LENGTH, 1))
    w_gate = centred(key_of[3], (EXPERTS, D, FF), D ** -0.5, 0.125, ((0, 4), (2, 32)))
    w_up = centred(key_of[4], (EXPERTS, D, FF), D ** -0.5, 0.125, ((0, 4), (2, 32)))
    w_down = centred(key_of[5], (EXPERTS, FF, D), FF ** -0.5, 0.0625, ((0, 4), (1, 32)))
    w_out = centred(key_of[6], (RECURRENT_LANES * P_SIZE, D), (RECURRENT_LANES * P_SIZE) ** -0.5, 0.09375, ((0, 4),))
    b_proj = centred(key_of[7], (SPAN_PARTITIONS, PIECE_LENGTH, N), 1.0, 6.0, ((0, 32),))
    c_proj = centred(key_of[8], (SPAN_PARTITIONS, PIECE_LENGTH, N), 0.003, 0.046875, ((0, 32),))
    log_decay = draw_log_decay(jax.random.fold_in(key_of[10], 71), 0)
    return dict(moe_input=moe_input, out_grad=out_grad, expert_id=expert_id, w_gate=w_gate, w_up=w_up, w_down=w_down, w_out=w_out, b_proj=b_proj, c_proj=c_proj, log_decay=log_decay)


def silu_parts(gate):
    logistic = jax.nn.sigmoid(gate)
    return (gate * logistic, logistic)

def shard_grad(decay, b_rows, c_rows, head_rows, carried):
    length = b_rows.shape[0]
    acum = jnp.cumsum(decay, axis=1)
    later = jnp.arange(length, dtype=jnp.int32)[:, None] >= jnp.arange(length, dtype=jnp.int32)[None, :]
    scores = lax.dot_general(c_rows, b_rows, (((1,), (1,)), ((), ())), preferred_element_type=jnp.float32)
    spread = acum[:, :, None] - acum[:, None, :]
    weight = jnp.where(later[None], jnp.exp(jnp.where(later[None], spread, 0.0)), 0.0) * scores[None]
    local = jnp.einsum('hts,thp->shp', weight, head_rows, precision=lax.Precision.HIGHEST)
    tail = jnp.exp(acum[:, -1:] - acum)
    cross = jnp.einsum('hs,sn,hnp->shp', tail, b_rows.astype(jnp.float32), carried, precision=lax.Precision.HIGHEST)
    weighted = jnp.exp(acum)
    summary = jnp.einsum('ht,tn,thp->hnp', weighted, c_rows.astype(jnp.float32), head_rows, precision=lax.Precision.HIGHEST)
    return (local + cross, summary, weighted[:, -1])

def reference(moe_input, out_grad, expert_id, w_gate, w_up, w_down, w_out, b_proj, c_proj, log_decay):
    blocks = SPAN_PARTITIONS * N_EXPERT
    rows = blocks * CAP
    slice_width = FF // N_SEQ
    flat_x = moe_input.reshape(blocks, TOK_DEV, D)
    flat_dy = out_grad.reshape(blocks, TOK_DEV, D)
    labels = expert_id.reshape(blocks, TOK_DEV)
    onehot = (labels[:, :, None] == jnp.arange(EXPERTS, dtype=jnp.int32)[None, None, :]).astype(jnp.int32)
    slot_index = lax.optimization_barrier(jnp.sum((jnp.cumsum(onehot, axis=1) - onehot) * onehot, axis=2))
    buffer_row = (jnp.arange(blocks, dtype=jnp.int32)[:, None] * CAP + slot_index).astype(jnp.int32)
    x_buffer = jnp.zeros((EXPERTS, rows, D), jnp.bfloat16).at[labels, buffer_row].set(flat_x)
    dy_buffer = jnp.zeros((EXPERTS, rows, D), jnp.bfloat16).at[labels, buffer_row].set(flat_dy)

    def one_expert(operands):
        x_rows, dy_rows, wg, wu, wd = operands
        gate = jnp.dot(x_rows, wg, preferred_element_type=jnp.float32)
        up = jnp.dot(x_rows, wu, preferred_element_type=jnp.float32)
        activated, logistic = silu_parts(gate)
        hidden = (activated * up).astype(jnp.bfloat16)
        hidden_grad = lax.dot_general(dy_rows, wd, (((1,), (1,)), ((), ())), preferred_element_type=jnp.float32)
        up_term = (hidden_grad * activated).astype(jnp.bfloat16)
        gate_term = (hidden_grad * up * logistic * (1.0 + gate * (1.0 - logistic))).astype(jnp.bfloat16)
        grad_g = lax.dot_general(x_rows, gate_term, (((0,), (0,)), ((), ())), preferred_element_type=jnp.float32)
        grad_u = lax.dot_general(x_rows, up_term, (((0,), (0,)), ((), ())), preferred_element_type=jnp.float32)
        grad_d = lax.dot_general(hidden, dy_rows, (((0,), (0,)), ((), ())), preferred_element_type=jnp.float32)
        gate_slices = gate_term.reshape(rows, N_SEQ, slice_width).transpose(1, 0, 2)
        up_slices = up_term.reshape(rows, N_SEQ, slice_width).transpose(1, 0, 2)
        wg_slices = wg.reshape(D, N_SEQ, slice_width).transpose(1, 0, 2)
        wu_slices = wu.reshape(D, N_SEQ, slice_width).transpose(1, 0, 2)

        def add_slice(total, pieces):
            g_part, u_part, wg_part, wu_part = pieces
            partial_sum = lax.dot_general(g_part, wg_part, (((1,), (1,)), ((), ())), preferred_element_type=jnp.float32)
            partial_sum = partial_sum + lax.dot_general(u_part, wu_part, (((1,), (1,)), ((), ())), preferred_element_type=jnp.float32)
            rounded = lax.optimization_barrier(partial_sum.astype(jnp.bfloat16))
            return (total + rounded.astype(jnp.float32), None)
        back_sum, _ = lax.scan(add_slice, jnp.zeros((rows, D), jnp.float32), (gate_slices, up_slices, wg_slices, wu_slices))
        return (back_sum.astype(jnp.bfloat16), grad_g, grad_u, grad_d)
    back_rows, gate_grad, up_grad, down_grad = lax.map(one_expert, (x_buffer, dy_buffer, w_gate, w_up, w_down))
    expert_grad = back_rows[labels, buffer_row]
    input_grad = (flat_dy.astype(jnp.float32) + expert_grad.astype(jnp.float32)).astype(jnp.bfloat16)
    grads_flat = out_grad.reshape(TOKENS, D)
    expert_flat = expert_grad.reshape(TOKENS, D)
    head_out = lax.dot_general(grads_flat, w_out, (((1,), (1,)), ((), ())), preferred_element_type=jnp.float32)
    head_out = head_out + lax.dot_general(expert_flat, w_out, (((1,), (1,)), ((), ())), preferred_element_type=jnp.float32)
    head_out = head_out.reshape(SPAN_PARTITIONS, PIECE_LENGTH, RECURRENT_LANES, P_SIZE)

    def shard_step(carried, pieces):
        decay, b_rows, c_rows, head_rows = pieces
        result, summary, total = shard_grad(decay, b_rows, c_rows, head_rows, carried)
        new_state = summary + total[:, None, None] * carried
        return (new_state, result.astype(jnp.bfloat16))
    _, head_grad = lax.scan(shard_step, jnp.zeros((RECURRENT_LANES, N, P_SIZE), jnp.float32), (log_decay, b_proj, c_proj, head_out), reverse=True)
    head_grad = head_grad.reshape(SPAN_PARTITIONS, PIECE_LENGTH, RECURRENT_LANES * P_SIZE)
    return (head_grad, input_grad.reshape(SPAN_PARTITIONS, PIECE_LENGTH, D), gate_grad, up_grad, down_grad)
```

```python
import jax
import jax.numpy as jnp
from jax import lax
from jax.sharding import Mesh
from jax.sharding import PartitionSpec as P

P_SIZE = 64
N = 128
CAP = 10
SLAB = 24
HALF = 4 * CAP
SEQ = ("seq_0", "seq_1", "seq_2")
F32 = jnp.float32
BF16 = jnp.bfloat16


def shift(a, axis, by):
    length = lax.axis_size(axis)
    return lax.ppermute(a, axis, [(i, (i + by) % length) for i in range(length)])


def total(*parts):
    result = parts[0].astype(F32)
    for part in parts[1:]:
        result = result + part.astype(F32)
    return result.astype(BF16)


def near(a, axis):
    return [a, shift(a, axis, 1), shift(a, axis, -1), shift(a, axis, 2)]


def far(a, axis):
    up, down = shift(a, axis, 1), shift(a, axis, -1)
    return up, down, (shift(up[0], axis, 1), shift(down[1], axis, -1))


def return_far(own, up, down, opposite, axis):
    half = opposite.shape[0] // 2
    first = shift(opposite[:half], axis, 1)
    second = shift(opposite[half:], axis, -1)
    down = total(down, jnp.pad(first, ((0, half), (0, 0))))
    up = total(up, jnp.pad(second, ((half, 0), (0, 0))))
    return total(own, shift(down, axis, 1), shift(up, axis, -1))


def return_near(blocks, axis, extra):
    own, up, down, opposite = blocks
    return total(
        own, shift(up, axis, -1), shift(down, axis, 1), shift(opposite, axis, 2), extra
    )


def silu_parts(gate):
    logistic = jax.nn.sigmoid(gate)
    return (gate * logistic, logistic)


def expert_chunk(x_rows, dy_rows, w_all, w_down):
    wide = jnp.dot(x_rows, w_all, preferred_element_type=F32)
    hidden_grad = lax.dot_general(
        dy_rows, w_down, (((1,), (1,)), ((), ())), preferred_element_type=F32
    )
    width = w_down.shape[0] // 2
    terms, hiddens = [], []
    for k in range(2):
        gate = wide[:, 2 * k * width : (2 * k + 1) * width]
        up = wide[:, (2 * k + 1) * width : (2 * k + 2) * width]
        grad = hidden_grad[:, k * width : (k + 1) * width]
        activated, logistic = silu_parts(gate)
        hiddens.append((activated * up).astype(BF16))
        terms.append((grad * up * logistic * (1.0 + gate * (1.0 - logistic))).astype(BF16))
        terms.append((grad * activated).astype(BF16))
    terms = jnp.concatenate(terms, axis=1)
    hidden = jnp.concatenate(hiddens, axis=1)
    partial = lax.dot_general(
        terms, w_all, (((1,), (1,)), ((), ())), preferred_element_type=F32
    ).astype(BF16)
    return terms, hidden, partial


def pick(array, index):
    return lax.dynamic_index_in_dim(array, index, 0, keepdims=False)


def body(moe_input, out_grad, expert_id, w_gate, w_up, w_down, w_out, b_proj, c_proj, log_decay):
    group, z, x, core = (lax.axis_index(name) for name in ("expert",) + SEQ)
    groups, zs, xs, cores = (lax.axis_size(name) for name in ("expert",) + SEQ)
    experts = groups * cores
    tokens, grads, labels = moe_input[0], out_grad[0], expert_id[0, :, 0]
    block, width = tokens.shape
    shards = zs * xs * cores

    other = 1 - core
    gate_up_sent = jnp.concatenate([pick(w_gate, other), pick(w_up, other)], axis=1)
    down_sent = pick(w_down, other)
    gate_up_got = shift(gate_up_sent, "seq_2", 1)
    down_got = shift(down_sent, "seq_2", 1)

    onehot = (labels[:, None] == jnp.arange(experts, dtype=jnp.int32)[None, :]).astype(jnp.int32)
    slot = jnp.sum((jnp.cumsum(onehot, axis=0) - onehot) * onehot, axis=1)
    code = labels * CAP + slot
    sent_row = jnp.arange(experts * SLAB, dtype=jnp.int32)[:, None]
    at_x = labels * SLAB + slot
    places = jnp.concatenate(
        [at_x, at_x + CAP, jnp.full((8,), -1, jnp.int32)], axis=0
    )
    meta = (jnp.arange(block + block + 8) == 2 * block)[None, :] & (
        sent_row % SLAB == 2 * CAP
    )
    placing = ((sent_row == places[None, :]) | meta).astype(BF16)
    meta_rows = jnp.zeros((8, width), BF16).at[0, :block].set(code.astype(BF16))
    sent = jnp.dot(
        placing, jnp.concatenate([tokens, grads, meta_rows], axis=0), preferred_element_type=F32
    ).astype(BF16)
    got = lax.all_to_all(
        sent.reshape(experts, SLAB, width),
        ("expert", "seq_2"),
        split_axis=0,
        concat_axis=0,
        tiled=True,
    )
    k = jnp.arange(2 * 2 * HALF, dtype=jnp.int32)
    source = ((k // CAP) % groups) * cores + k // (2 * HALF)
    wanted = source * SLAB + ((k // HALF) % 2) * CAP + k % CAP
    gathering = (wanted[:, None] == jnp.arange(experts * SLAB, dtype=jnp.int32)[None, :]).astype(BF16)
    rows = (
        jnp.dot(gathering, got.reshape(experts * SLAB, width), preferred_element_type=F32)
        .astype(BF16)
        .reshape(2, 2, HALF, width)
    )
    codes = pick(got[:, 2 * CAP, :block].reshape(groups, cores, block).transpose(1, 0, 2), core)

    decay = log_decay[0]
    heads = decay.shape[0]
    length = decay.shape[1]
    acum = jnp.cumsum(decay, axis=1)
    totals = lax.all_to_all(
        jnp.broadcast_to(acum[None, None, :, -1], (shards, 1, heads)),
        SEQ,
        split_axis=0,
        concat_axis=0,
        tiled=True,
    )[:, 0, :]

    a_near = jnp.concatenate(near(rows[0], "seq_1"), axis=1)
    b_near = jnp.concatenate(near(rows[1], "seq_0"), axis=1)
    a_up, a_down, a_opposite = far(a_near, "seq_0")
    b_up, b_down, b_opposite = far(b_near, "seq_1")

    own_gate_up = jnp.concatenate([pick(w_gate, core), pick(w_up, core)], axis=1)
    w_all = jnp.concatenate([own_gate_up, gate_up_got], axis=1)
    w_down_all = jnp.concatenate([pick(w_down, core), down_got], axis=0)
    part = a_near.shape[1]

    def chunk(xs_, dys_):
        x_rows = jnp.concatenate(xs_, axis=0)
        dy_rows = jnp.concatenate(dys_, axis=0)
        return (x_rows, dy_rows) + expert_chunk(x_rows, dy_rows, w_all, w_down_all)

    first = chunk([a_near[0], b_near[0]], [a_near[1], b_near[1]])
    second = chunk(
        [a_up[0], a_down[0], b_up[0], b_down[0]], [a_up[1], a_down[1], b_up[1], b_down[1]]
    )
    third = chunk([a_opposite[0], b_opposite[0]], [a_opposite[1], b_opposite[1]])

    own_p, side_p, opp_p = first[4], second[4], third[4]
    a_sum = return_far(
        own_p[:part], side_p[:part], side_p[part : 2 * part], opp_p[:part], "seq_0"
    )
    b_sum = return_far(
        own_p[part:], side_p[2 * part : 3 * part], side_p[3 * part :], opp_p[part:], "seq_1"
    )
    a_rows = return_near(list(a_sum.reshape(4, HALF, width)), "seq_1", rows[0, 1])
    b_rows_ = return_near(list(b_sum.reshape(4, HALF, width)), "seq_0", rows[1, 1])

    x_all, dy_all, terms, hidden = (
        jnp.concatenate([c[i] for c in (first, second, third)], axis=0) for i in range(4)
    )
    ff = w_gate.shape[2]

    def grads_of(lhs, rhs):
        return lax.dot_general(lhs, rhs, (((0,), (0,)), ((), ())), preferred_element_type=F32)

    gu_sent = grads_of(x_all, terms[:, 2 * ff :]).astype(BF16)
    d_sent = grads_of(hidden[:, ff:], dy_all).astype(BF16)
    gu_got = shift(gu_sent, "seq_2", 1)
    d_got = shift(d_sent, "seq_2", 1)
    gu_own = grads_of(x_all, terms[:, : 2 * ff])
    d_own = grads_of(hidden[:, :ff], dy_all)

    def in_order(own, got_):
        got_ = got_.astype(F32)
        return jnp.stack([jnp.where(core == 0, own, got_), jnp.where(core == 0, got_, own)])

    grad_gate = in_order(gu_own[:, :ff], gu_got[:, :ff])
    grad_up = in_order(gu_own[:, ff:], gu_got[:, ff:])
    grad_down = in_order(d_own, d_got)

    kept = jnp.where(core == 0, a_rows, b_rows_)
    given = jnp.where(core == 0, b_rows_, a_rows)
    pair = jnp.concatenate([kept, shift(given, "seq_2", 1)], axis=0)
    y_up, y_down = shift(pair, "expert", 1), shift(pair, "expert", -1)
    everything = jnp.concatenate(
        [pair, y_up, y_down, shift(y_up[:HALF], "expert", 1), shift(y_down[HALF:], "expert", -1)],
        axis=0,
    )
    r = jnp.arange(8 * HALF, dtype=jnp.int32)
    offset = jnp.array([0, 1, 3, 2], jnp.int32)
    row_group = (group - jnp.repeat(offset, 2 * HALF) + groups) % groups
    row_core = jnp.where((r // HALF) % 2 == 0, core, other)
    row_code = ((r // CAP) % groups) * (experts * CAP) + (
        row_group * cores + row_core
    ) * CAP + r % CAP
    token_code = (
        codes.astype(jnp.int32)
        + (jnp.arange(groups, dtype=jnp.int32) * (experts * CAP))[:, None]
    ).reshape(-1)
    choosing = (token_code[:, None] == row_code[None, :]).astype(BF16)
    shard_grad = jnp.dot(choosing, everything, preferred_element_type=F32).astype(BF16)
    input_grad = lax.dynamic_slice_in_dim(shard_grad, group * block, block, 0)

    head_rows = lax.dot_general(
        shard_grad, w_out, (((1,), (1,)), ((), ())), preferred_element_type=F32
    )
    b_mat, c_mat = b_proj[0], c_proj[0]
    decay_t = jnp.repeat(acum.T, P_SIZE, axis=1)
    weighted = (jnp.exp(decay_t) * head_rows).astype(BF16)
    summary = lax.dot_general(
        c_mat, weighted, (((0,), (0,)), ((), ())), preferred_element_type=F32
    ).astype(BF16)

    here = (z * xs + x) * cores + core
    chip = here - core
    row0 = z * xs * cores
    s = jnp.arange(shards, dtype=jnp.int32)

    def between(low, high):
        inside = ((s >= low) & (s < high)).astype(F32)
        log = jnp.sum(inside[:, None] * totals, axis=0)
        return jnp.repeat(jnp.exp(log), P_SIZE)[None, :]

    half_n = N // 2
    partner = shift(summary, "seq_2", 1)

    def own_half(a):
        return jnp.where(core == 0, a[:half_n], a[half_n:]).astype(F32)

    mine_half, partner_half = own_half(summary), own_half(partner)
    chip_state = jnp.where(core == 0, mine_half, partner_half) + between(chip, chip + 1) * jnp.where(
        core == 0, partner_half, mine_half
    )
    chip_sent = chip_state.astype(BF16)
    later_x = jnp.zeros_like(chip_state)
    row_state = between(row0, chip) * chip_state
    for step in range(1, 4):
        part_state = shift(chip_sent, "seq_1", -step).astype(F32)
        at = (x + step) % xs
        start = row0 + at * cores
        row_state = row_state + between(row0, start) * part_state
        later_x = later_x + jnp.where(at > x, between(chip + cores, start), 0.0) * part_state
    row_sent = row_state.astype(BF16)
    later_z = jnp.zeros_like(chip_state)
    for step in range(1, 4):
        part_state = shift(row_sent, "seq_0", -step).astype(F32)
        at = (z + step) % zs
        start = at * xs * cores
        later_z = later_z + jnp.where(at > z, between(row0 + xs * cores, start), 0.0) * part_state
    chip_carried = later_x + between(chip + cores, row0 + xs * cores) * later_z
    carried_sent = chip_carried.astype(BF16)
    carried_got = shift(carried_sent, "seq_2", 1)
    outer = jnp.concatenate(
        [
            jnp.where(core == 0, carried_sent, carried_got),
            jnp.where(core == 0, carried_got, carried_sent),
        ],
        axis=0,
    ).astype(F32)
    carried = between(here + 1, chip + cores) * outer + jnp.where(
        core == 0, partner.astype(F32), 0.0
    )

    later = (
        jnp.arange(length, dtype=jnp.int32)[:, None] >= jnp.arange(length, dtype=jnp.int32)[None, :]
    )
    scores = lax.dot_general(
        c_mat, b_mat, (((1,), (1,)), ((), ())), preferred_element_type=F32
    )
    spread = acum[:, :, None] - acum[:, None, :]
    weight = (
        jnp.where(later[None], jnp.exp(jnp.where(later[None], spread, 0.0)), 0.0) * scores[None]
    ).astype(BF16)
    local = jnp.einsum(
        "hts,thp->shp",
        weight,
        head_rows.astype(BF16).reshape(length, heads, P_SIZE),
        preferred_element_type=F32,
    ).reshape(length, heads * P_SIZE)
    tail = jnp.exp(decay_t[-1:] - decay_t)
    cross = tail * jnp.dot(b_mat, carried.astype(BF16), preferred_element_type=F32)
    head_grad = (local + cross).astype(BF16)
    return (head_grad[None], input_grad[None], grad_gate, grad_up, grad_down)


def solution(mesh):
    finer = Mesh(
        mesh.devices.reshape(mesh.shape["expert"], 4, 4, 2), ("expert", "seq_0", "seq_1", "seq_2")
    )
    return jax.shard_map(
        body,
        mesh=finer,
        in_specs=(
            P(SEQ, "expert", None),
            P(SEQ, "expert", None),
            P(SEQ, "expert", None),
            P("expert", None, SEQ),
            P("expert", None, SEQ),
            P("expert", SEQ, None),
            P("expert", None),
            P(SEQ, None, None),
            P(SEQ, None, None),
            P(SEQ, "expert", None),
        ),
        out_specs=(
            P(SEQ, None, "expert"),
            P(SEQ, "expert", None),
            P("expert", None, SEQ),
            P("expert", None, SEQ),
            P("expert", SEQ, None),
        ),
        check_vma=False,
    )
```
